32 devices in a mesh: teacher: 4 (over y, x), student: 8 (over z, core).
Axes of the slice: x: 2, y: 2, z: 4, core: 2. Of those that a mesh axis runs over, the one named last changes fastest.
Arguments:
- teacher_in: bfloat16 [8192, 8192], P('student', 'teacher')
- teacher_attn: bfloat16 [8192, 4096], P('student', 'teacher'), may hold values from -6 to 6
- teacher_out_proj: bfloat16 [4096, 8192], P('student', 'teacher'), may hold values from -0.09375 to 0.09375
- teacher_gain: bfloat16 [8192], P('teacher'), may hold values from 0.099609375 to 1.8984375
- projection: bfloat16 [8192, 4096], P('teacher', 'student'), may hold values from -0.0625 to 0.0625
- student_in: bfloat16 [8192, 4096], P('student', 'teacher')
- student_attn: bfloat16 [8192, 2048], P('student', 'teacher'), may hold values from -6 to 6
- student_out_proj: bfloat16 [2048, 4096], P('student', 'teacher'), may hold values from -0.125 to 0.125
- student_gain: bfloat16 [4096], P('teacher'), may hold values from 0.099609375 to 1.8984375
- token_ids: int32 [8192], P('student'), may hold values from 0 to 128004, as said below
- row_order: int32 [8192], replicated, may hold values from 0 to 8191, as said below
Outputs:
- grad_weight: float32 [2048, 4096], P('student', 'teacher')
- grad_gain: float32 [4096], P('teacher')
The draws below stay inside these ranges and needn't reach their ends.
Inputs may be any that keep to these rules, and one draw needn't show every extreme that they name: `token_ids`: within each sequence of 1024 consecutive rows the rows holding 128004 form the sequence's tail, after at least 256 other rows; no other row holds 128004. `row_order`: A permutation of the 8192 rows. For student block k and teacher block b (blocks of 1024 rows), the entries k * 1024 + b * 128 to k * 1024 + (b + 1) * 128 - 1 name rows of teacher block b.
All inputs are finite; a program needn't handle non-finite values.
Results may differ from the reference program's by a relative error of at most 0.02.
Values may be sent and summed in bfloat16 or wider, within the bound.
No kernel may reach another device: no remote copies, remote signals or barrier semaphores. Data moves between devices by JAX's collectives and lax.ppermute only.
A program may use at most 128 MiB of HBM per device.

```python
import jax
import jax.numpy as jnp
from jax import lax

DT = 8192
DS = 4096
HEAD = 128
HT = 32
HS = 16
SEQ = 1024
PAD_ID = 128004
GROUP_ROWS = 1024
TOKENS = 8192
PIECE = 128
N_TEACHER = 4


def scaled_rows(key, row_count, column_count):
    first_key, second_key = jax.random.split(key, 2)
    normal_base = jax.random.normal(first_key, (row_count, column_count), jnp.float32)
    column_ramp = jnp.arange(column_count, dtype=jnp.float32) / column_count
    jitter = jnp.exp(0.3 * jax.random.normal(second_key, (column_count,), jnp.float32))
    column_scale = jnp.exp(jnp.log(5.0) * column_ramp) * jitter
    return normal_base * column_scale[None, :]


def draw_teacher_in(key, part):
    return scaled_rows(jax.random.fold_in(key, 11), TOKENS, DT).astype(jnp.bfloat16)


def draw_student_in(key, part):
    return scaled_rows(jax.random.fold_in(key, 23), TOKENS, DS).astype(jnp.bfloat16)


def draw_token_ids(key, part):
    first_key, second_key = jax.random.split(jax.random.fold_in(key, 37))
    sequence_count = TOKENS // SEQ
    live_len = jax.random.randint(first_key, (sequence_count, 1), SEQ // 4, SEQ + 1)
    word_ids = jax.random.randint(second_key, (sequence_count, SEQ), 0, PAD_ID)
    position = jnp.arange(SEQ)[None, :]
    return jnp.where(position < live_len, word_ids, PAD_ID).reshape(TOKENS).astype(jnp.int32)


def draw_row_order(key, part):
    block_count = TOKENS // GROUP_ROWS
    block_keys = jax.random.split(jax.random.fold_in(key, 41), block_count)
    shuffled = jax.vmap(lambda one_key: jax.random.permutation(one_key, GROUP_ROWS))(block_keys)
    shuffled = shuffled + (jnp.arange(block_count) * GROUP_ROWS)[:, None]
    shuffled = shuffled.reshape(block_count, block_count, PIECE)
    return jnp.transpose(shuffled, (1, 0, 2)).reshape(TOKENS).astype(jnp.int32)


def strengthened(array, own_key, source, target, parts, factor):
    def block_of(axis_at):
        return (jnp.arange(array.shape[axis_at]) // (array.shape[axis_at] // parts)).reshape((-1,) + (1,) * (array.ndim - 1 - axis_at))

    one_side = jax.random.permutation(own_key, parts)[block_of(target)]
    second = (block_of(target) + parts // 2) % parts
    return jnp.where((block_of(source) == one_side) | (block_of(source) == second), factor * array, array)


def level_of(rng, extent, cuts, least, largest):
    gain, own = 1.0, jax.random.fold_in(rng, 6)
    for dim, blocks in cuts:
        heights = jnp.exp(jax.random.uniform(jax.random.fold_in(own, dim), (blocks,), jnp.float32, least / len(cuts), largest / len(cuts)))
        gain = gain * jnp.repeat(heights, extent[dim] // blocks).reshape([-1 if axis == dim else 1 for axis in range(len(extent))])
    return gain


def normal_values(stream_key, shape, width, bound, pieces=(), kind=jnp.bfloat16):
    result = width * jax.random.normal(stream_key, shape, jnp.float32)
    if pieces:
        result = result * level_of(stream_key, shape, pieces, -0.22, 0.18)
    return jnp.clip(result, -bound, bound).astype(kind)


def gaussian_with(stream_key, shape, scale, bound, pieces, heavy, held_as=jnp.bfloat16):
    values = scale * jax.random.normal(stream_key, shape, jnp.float32)
    if pieces:
        values = values * level_of(stream_key, shape, pieces, -0.22, 0.18)
    return jnp.clip(strengthened(values, jax.random.fold_in(stream_key, 3), *heavy), -bound, bound).astype(held_as)


def setup_inputs(seed: int = 0) -> dict:
    key_list = jax.random.split(jax.random.key(seed), 12)
    return {
        "teacher_in": draw_teacher_in(jax.random.fold_in(key_list[11], 71), 0),
        "teacher_attn": normal_values(key_list[1], (TOKENS, HT * HEAD), 1.0, 6.0, ((0, 8), (1, 4))),
        "teacher_out_proj": normal_values(key_list[2], (HT * HEAD, DT), (HT * HEAD) ** -0.5, 0.09375, ((0, 8), (1, 4))),
        "teacher_gain": jnp.clip(1.0 + 0.18 * jax.random.normal(key_list[3], (DT,), jnp.float32), 0.099609375, 1.8984375).astype(jnp.bfloat16),
        "projection": normal_values(key_list[4], (DT, DS), DT ** -0.5, 0.0625, ((0, 4), (1, 8))),
        "student_in": draw_student_in(jax.random.fold_in(key_list[11], 71), 0),
        "student_attn": gaussian_with(key_list[6], (TOKENS, HS * HEAD), 1.0, 6.0, ((0, 8), (1, 4)), (0, 1, 8, 2.0)),
        "student_out_proj": normal_values(key_list[7], (HS * HEAD, DS), (HS * HEAD) ** -0.5, 0.125, ((0, 8), (1, 4))),
        "student_gain": jnp.clip(1.0 + 0.18 * jax.random.normal(key_list[8], (DS,), jnp.float32), 0.099609375, 1.8984375).astype(jnp.bfloat16),
        "token_ids": draw_token_ids(jax.random.fold_in(key_list[11], 71), 0),
        "row_order": draw_row_order(jax.random.fold_in(key_list[11], 71), 0),
    }


epsilon = 1e-05

def reference(teacher_in, teacher_attn, teacher_out_proj, teacher_gain, projection, student_in, student_attn, student_out_proj, student_gain, token_ids, row_order):
    residual = teacher_in.astype(jnp.float32) + jnp.dot(teacher_attn, teacher_out_proj, preferred_element_type=jnp.float32)
    teacher_scale = lax.rsqrt(lax.optimization_barrier(jnp.mean(residual * residual, axis=1, keepdims=True)) + epsilon)
    hidden = (residual * teacher_scale * teacher_gain.astype(jnp.float32)).astype(jnp.bfloat16)
    block_width = DT // N_TEACHER
    summed = jnp.zeros((TOKENS, DS), jnp.float32)
    for block in range(N_TEACHER):
        lower = block * block_width
        partial_term = jnp.dot(hidden[:, lower:lower + block_width], projection[lower:lower + block_width], preferred_element_type=jnp.float32)
        rounded = lax.optimization_barrier(partial_term.astype(jnp.bfloat16))
        summed = summed + rounded.astype(jnp.float32)
    target = summed.astype(jnp.bfloat16)
    live_rows = jnp.where(token_ids != PAD_ID, 1.0, 0.0).astype(jnp.float32)
    target_s = jnp.take(target, row_order, axis=0).astype(jnp.float32)
    live_s = jnp.take(live_rows, row_order, axis=0)
    student_res = student_in.astype(jnp.float32) + jnp.dot(student_attn, student_out_proj, preferred_element_type=jnp.float32)
    student_scale = lax.rsqrt(lax.optimization_barrier(jnp.mean(student_res * student_res, axis=1, keepdims=True)) + epsilon)
    normed = student_res * student_scale
    gain_values = student_gain.astype(jnp.float32)
    distance = normed * gain_values - target_s
    loss_weight = 1.0 / jnp.sqrt(jnp.float32(TOKENS))
    grad_out = distance * (live_s * loss_weight)[:, None]
    grad_gain = lax.optimization_barrier(jnp.sum(grad_out * normed, axis=0))
    grad_norm = grad_out * gain_values
    inner = lax.optimization_barrier(jnp.mean(grad_norm * normed, axis=1, keepdims=True))
    grad_res = (student_scale * (grad_norm - normed * inner)).astype(jnp.bfloat16)
    grad_weight = jnp.dot(student_attn.T, grad_res, preferred_element_type=jnp.float32)
    return (grad_weight, grad_gain)
```

```python
import math

import jax
import jax.numpy as jnp
from jax import lax
from jax.sharding import PartitionSpec as P

PAD_ID = 128004
epsilon = 1e-05
BF, F32 = jnp.bfloat16, jnp.float32


def after(value, *others):
    return lax.optimization_barrier((value, *others))[0]


def fan_out(block, teachers):
    return [block] + [
        lax.ppermute(block, "teacher", [(i, i ^ j) for i in range(teachers)])
        for j in range(1, teachers)
    ]


def teacher_sum(value, teachers):
    got = fan_out(value, teachers)
    total = got[0]
    for part in got[1:]:
        total = total + part
    return total


def core_swap(block, students):
    return lax.ppermute(block, "student", [(i, i ^ 1) for i in range(students)])


def line_gather(block, students, chip):
    chips = students // 2
    up, down = [block], [block]
    for step in range(1, chips):
        up.append(
            lax.ppermute(
                up[-1],
                "student",
                [(2 * q + c, 2 * q + 2 + c) for q in range(step - 1, chips - 1) for c in range(2)],
            )
        )
        down.append(
            lax.ppermute(
                down[-1],
                "student",
                [(2 * q + c, 2 * q - 2 + c) for q in range(1, chips - step + 1) for c in range(2)],
            )
        )
    got = [(chip, block, core_swap(block, students))]
    for step in range(1, chips):
        mine = jnp.where(chip >= step, up[step], down[chips - step])
        got.append((lax.rem(chip - step + chips, chips), mine, core_swap(mine, students)))
    return got


def shards(
    teacher_in,
    teacher_attn,
    teacher_out_proj,
    teacher_gain,
    projection,
    student_in,
    student_attn,
    student_out_proj,
    student_gain,
    token_ids,
    row_order,
):
    students = lax.axis_size("student")
    teachers = lax.axis_size("teacher")
    ratio = students // teachers
    rows = teacher_in.shape[0]
    piece = rows // students
    s = lax.axis_index("student")
    t = lax.axis_index("teacher")
    chip, core = s // 2, lax.rem(s, 2)
    width_t = teacher_in.shape[1] * teachers
    width_s = student_in.shape[1] * teachers

    def place(who):
        return ratio * (t ^ (who // ratio)) + lax.rem(who, ratio)

    def assemble(blocks):
        full = jnp.zeros((students, *blocks[0][1].shape), BF)
        for q, mine, other in blocks:
            full = lax.dynamic_update_index_in_dim(full, mine, place(2 * q + core), 0)
            full = lax.dynamic_update_index_in_dim(full, other, place(2 * q + 1 - core), 0)
        return full

    student_attn_all = jnp.concatenate(fan_out(student_attn, teachers), axis=1)
    student_proj = assemble(line_gather(student_out_proj, students, chip))
    attn_all = jnp.concatenate(fan_out(teacher_attn, teachers), axis=1)
    half = teacher_out_proj.shape[0] // 2
    out_blocks = [
        line_gather(teacher_out_proj[i * half : (i + 1) * half], students, chip) for i in range(2)
    ]
    out_proj = jnp.concatenate([assemble(b) for b in out_blocks], axis=1)

    student_res = student_in.astype(F32) + jnp.dot(
        student_attn_all, student_proj.reshape(-1, student_proj.shape[2]), preferred_element_type=F32
    )
    student_square = teacher_sum(jnp.sum(student_res * student_res, axis=1), teachers)
    student_scale = lax.rsqrt(student_square / width_s + epsilon)
    normed = student_res * student_scale[:, None]
    gain_values = student_gain.astype(F32)[None, :]

    row_blocks = row_order.reshape(students, students, piece)
    local_rows = lax.dynamic_index_in_dim(row_blocks, s, 1, keepdims=False) - s * rows
    chosen = local_rows.reshape(rows)[:, None] == jnp.arange(rows, dtype=jnp.int32)[None, :]
    live = token_ids != PAD_ID
    mask_send = jnp.max(jnp.where(chosen & live[None, :], 1.0, 0.0), axis=1).astype(BF)
    select = chosen.astype(BF)
    mask = lax.all_to_all(
        mask_send.reshape(students, 1, piece), "student", split_axis=0, concat_axis=0, tiled=True
    )
    weight_mask = mask.reshape(rows).astype(F32)

    residual = teacher_in.astype(F32) + jnp.dot(
        attn_all, out_proj.reshape(-1, out_proj.shape[2]), preferred_element_type=F32
    )
    square_sum = teacher_sum(jnp.sum(residual * residual, axis=1), teachers)
    teacher_scale = lax.rsqrt(square_sum / width_t + epsilon)
    hidden = (residual * teacher_scale[:, None] * teacher_gain.astype(F32)[None, :]).astype(BF)

    projection_t = projection.T
    chunk = 128
    pieces = []
    gate = out_blocks[-1][2][1]
    for start in range(0, projection_t.shape[0], chunk):
        block = after(projection_t[start : start + chunk], gate)
        blocks = line_gather(block, students, chip)
        gate = blocks[2][1] if len(blocks) > 2 else blocks[-1][1]
        columns = assemble(blocks)
        parts = [
            lax.dot_general(
                hidden,
                columns[ratio * j : ratio * (j + 1)].reshape(ratio * chunk, -1),
                (((1,), (1,)), ((), ())),
                preferred_element_type=F32,
            ).astype(BF)
            for j in range(teachers)
        ]
        total = parts[0].astype(F32)
        for j in range(1, teachers):
            total = total + lax.ppermute(
                parts[j], "teacher", [(i, i ^ j) for i in range(teachers)]
            ).astype(F32)
        picked = jnp.dot(select, total.astype(BF), preferred_element_type=F32).astype(BF)
        moved = lax.all_to_all(
            picked.reshape(students, piece, ratio * chunk),
            "student",
            split_axis=0,
            concat_axis=0,
            tiled=True,
        )
        pieces.append(moved.reshape(rows, ratio * chunk))
    target = jnp.concatenate(
        [p[:, u * chunk : (u + 1) * chunk] for u in range(ratio) for p in pieces], axis=1
    )

    distance = normed * gain_values - target.astype(F32)
    loss_weight = 1.0 / math.sqrt(rows * students)
    grad_out = distance * (weight_mask * loss_weight)[:, None]
    gain_part = jnp.sum(grad_out * normed, axis=0)
    grad_norm = grad_out * gain_values
    inner_sum = teacher_sum(jnp.sum(grad_norm * normed, axis=1), teachers)
    grad_res = (student_scale[:, None] * (grad_norm - normed * (inner_sum / width_s)[:, None])).astype(BF)
    grad_gain = gain_part
    for bit in range(students.bit_length() - 1):
        grad_gain = grad_gain + lax.ppermute(
            grad_gain, "student", [(i, i ^ (1 << bit)) for i in range(students)]
        )
    partial = lax.dot_general(
        student_attn_all, grad_res, (((0,), (0,)), ((), ())), preferred_element_type=F32
    ).astype(BF)
    partial = partial.reshape(students, -1, partial.shape[1])
    chips = students // 2
    total = jnp.zeros(partial.shape[1:], F32)
    for step in range(chips):
        q = chip ^ step
        mine = lax.dynamic_index_in_dim(partial, place(2 * q + core), 0, keepdims=False)
        other = lax.dynamic_index_in_dim(partial, place(2 * q + 1 - core), 0, keepdims=False)
        pair = mine.astype(F32) + core_swap(other, students).astype(F32)
        if step:
            pair = lax.ppermute(
                pair.astype(BF), "student", [(i, i ^ (2 * step)) for i in range(students)]
            ).astype(F32)
        total = total + pair
    return (total, grad_gain)


def solution(mesh):
    placed = (
        P("student", "teacher"),
        P("student", "teacher"),
        P("student", "teacher"),
        P("teacher"),
        P("teacher", "student"),
        P("student", "teacher"),
        P("student", "teacher"),
        P("student", "teacher"),
        P("teacher"),
        P("student"),
        P(),
    )
    return jax.shard_map(
        shards,
        mesh=mesh,
        in_specs=placed,
        out_specs=(P("student", "teacher"), P("teacher")),
        check_vma=False,
    )
```

```python
import math

import jax
import jax.numpy as jnp
from jax import lax
from jax.experimental import pallas as pl
from jax.experimental.pallas import tpu as pltpu
from jax.sharding import PartitionSpec as P


PAD_ID = 128004
epsilon = 1e-05
BF, F32 = jnp.bfloat16, jnp.float32

NF, NC = 2, 2


def after(value, *others):
    return lax.optimization_barrier((value, *others))[0]


def fan_out(block, teachers):
    return [block] + [
        lax.ppermute(block, "teacher", [(i, i ^ j) for i in range(teachers)])
        for j in range(1, teachers)
    ]


def teacher_sum(value, teachers):
    got = fan_out(value, teachers)
    total = got[0]
    for part in got[1:]:
        total = total + part
    return total


def core_swap(block, students):
    return lax.ppermute(block, "student", [(i, i ^ 1) for i in range(students)])


def line_gather(block, students, chip):
    chips = students // 2
    up, down = [block], [block]
    for step in range(1, chips):
        up.append(
            lax.ppermute(
                up[-1],
                "student",
                [(2 * q + c, 2 * q + 2 + c) for q in range(step - 1, chips - 1) for c in range(2)],
            )
        )
        down.append(
            lax.ppermute(
                down[-1],
                "student",
                [(2 * q + c, 2 * q - 2 + c) for q in range(1, chips - step + 1) for c in range(2)],
            )
        )
    got = [(chip, block, core_swap(block, students))]
    for step in range(1, chips):
        mine = jnp.where(chip >= step, up[step], down[chips - step])
        got.append((lax.rem(chip - step + chips, chips), mine, core_swap(mine, students)))
    return got


def shards(
    teacher_in,
    teacher_attn,
    teacher_out_proj,
    teacher_gain,
    projection,
    student_in,
    student_attn,
    student_out_proj,
    student_gain,
    token_ids,
    row_order,
):
    students = lax.axis_size("student")
    teachers = lax.axis_size("teacher")
    ratio = students // teachers
    rows = teacher_in.shape[0]
    piece = rows // students
    s = lax.axis_index("student")
    t = lax.axis_index("teacher")
    chip, core = s // 2, lax.rem(s, 2)
    width_t = teacher_in.shape[1] * teachers
    width_s = student_in.shape[1] * teachers

    def place(who):
        return ratio * (t ^ (who // ratio)) + lax.rem(who, ratio)

    def assemble(blocks):
        full = jnp.zeros((students, *blocks[0][1].shape), BF)
        for q, mine, other in blocks:
            full = lax.dynamic_update_index_in_dim(full, mine, place(2 * q + core), 0)
            full = lax.dynamic_update_index_in_dim(full, other, place(2 * q + 1 - core), 0)
        return full

    student_attn_all = jnp.concatenate(fan_out(student_attn, teachers), axis=1)
    student_proj = assemble(line_gather(student_out_proj, students, chip))
    attn_all = jnp.concatenate(fan_out(teacher_attn, teachers), axis=1)
    half = teacher_out_proj.shape[0] // 2
    out_blocks = [
        line_gather(teacher_out_proj[i * half : (i + 1) * half], students, chip) for i in range(2)
    ]
    out_proj = jnp.concatenate([assemble(b) for b in out_blocks], axis=1)

    student_res = student_in.astype(F32) + jnp.dot(
        student_attn_all, student_proj.reshape(-1, student_proj.shape[2]), preferred_element_type=F32
    )
    student_square = teacher_sum(jnp.sum(student_res * student_res, axis=1), teachers)
    student_scale = lax.rsqrt(student_square / width_s + epsilon)
    normed = student_res * student_scale[:, None]
    gain_values = student_gain.astype(F32)[None, :]

    row_blocks = row_order.reshape(students, students, piece)
    local_rows = lax.dynamic_index_in_dim(row_blocks, s, 1, keepdims=False) - s * rows
    chosen = local_rows.reshape(rows)[:, None] == jnp.arange(rows, dtype=jnp.int32)[None, :]
    live = token_ids != PAD_ID
    mask_send = jnp.max(jnp.where(chosen & live[None, :], 1.0, 0.0), axis=1).astype(BF)
    select = chosen.astype(BF)
    mask = lax.all_to_all(
        mask_send.reshape(students, 1, piece), "student", split_axis=0, concat_axis=0, tiled=True
    )
    weight_mask = mask.reshape(rows).astype(F32)

    residual = teacher_in.astype(F32) + jnp.dot(
        attn_all, out_proj.reshape(-1, out_proj.shape[2]), preferred_element_type=F32
    )
    square_sum = teacher_sum(jnp.sum(residual * residual, axis=1), teachers)
    teacher_scale = lax.rsqrt(square_sum / width_t + epsilon)
    hidden = (residual * teacher_scale[:, None] * teacher_gain.astype(F32)[None, :]).astype(BF)

    projection_t = projection.T
    chunk = 128
    pieces = []
    gate = out_blocks[-1][2][1]
    for start in range(0, projection_t.shape[0], chunk):
        block = after(projection_t[start : start + chunk], gate)
        blocks = line_gather(block, students, chip)
        gate = blocks[2][1] if len(blocks) > 2 else blocks[-1][1]
        columns = assemble(blocks)
        parts = [
            lax.dot_general(
                hidden,
                columns[ratio * j : ratio * (j + 1)].reshape(ratio * chunk, -1),
                (((1,), (1,)), ((), ())),
                preferred_element_type=F32,
            ).astype(BF)
            for j in range(teachers)
        ]
        total = parts[0].astype(F32)
        for j in range(1, teachers):
            total = total + lax.ppermute(
                parts[j], "teacher", [(i, i ^ j) for i in range(teachers)]
            ).astype(F32)
        picked = jnp.dot(select, total.astype(BF), preferred_element_type=F32).astype(BF)
        moved = lax.all_to_all(
            picked.reshape(students, piece, ratio * chunk),
            "student",
            split_axis=0,
            concat_axis=0,
            tiled=True,
        )
        pieces.append(moved.reshape(rows, ratio * chunk))
    target = jnp.concatenate(
        [p[:, u * chunk : (u + 1) * chunk] for u in range(ratio) for p in pieces], axis=1
    )

    distance = normed * gain_values - target.astype(F32)
    loss_weight = 1.0 / math.sqrt(rows * students)
    grad_out = distance * (weight_mask * loss_weight)[:, None]
    gain_part = jnp.sum(grad_out * normed, axis=0)
    grad_norm = grad_out * gain_values
    inner_sum = teacher_sum(jnp.sum(grad_norm * normed, axis=1), teachers)
    grad_res = (student_scale[:, None] * (grad_norm - normed * (inner_sum / width_s)[:, None])).astype(BF)
    grad_gain = gain_part
    for bit in range(students.bit_length() - 1):
        grad_gain = grad_gain + lax.ppermute(
            grad_gain, "student", [(i, i ^ (1 << bit)) for i in range(students)]
        )
    partial = lax.dot_general(
        student_attn_all, grad_res, (((0,), (0,)), ((), ())), preferred_element_type=F32
    ).astype(BF)
    partial = partial.reshape(students, -1, partial.shape[1])
    chips = students // 2
    total = jnp.zeros(partial.shape[1:], F32)
    for step in range(chips):
        q = chip ^ step
        mine = lax.dynamic_index_in_dim(partial, place(2 * q + core), 0, keepdims=False)
        other = lax.dynamic_index_in_dim(partial, place(2 * q + 1 - core), 0, keepdims=False)
        pair = mine.astype(F32) + core_swap(other, students).astype(F32)
        if step:
            pair = lax.ppermute(
                pair.astype(BF), "student", [(i, i ^ (2 * step)) for i in range(students)]
            ).astype(F32)
        total = total + pair
    return (total, grad_gain)


def near_far(chip, left, right):
    return jnp.where(chip < 2, left, right)


DEAD = 2.0**100


def residual_kernel(s_ref, a0, a1, a2, a3, in_ref, gain_ref, *rest):
    own, one, two, three, one_out, two_out, three_out = rest[:7]
    hidden_ref, square_ref, held, sems = rest[-4:]

    def copy(k, ref):
        return pltpu.make_async_copy(ref, held.at[s_ref[k]], sems.at[k])

    @pl.when(pl.program_id(0) == 0)
    def _():
        copy(0, own).start()

        @pl.when(s_ref[4] == 1)
        def _():
            for k, ref in enumerate((one, two, three)):
                copy(k + 1, ref).start()

        @pl.when(s_ref[4] == 0)
        def _():
            for k, ref in enumerate((one_out, two_out, three_out)):
                copy(k + 1, ref).start()

        for k in range(4):
            copy(k, own).wait()

    total = in_ref[...].astype(F32)
    for k, a in enumerate((a0, a1, a2, a3)):
        total = total + jnp.dot(a[...], held[k], preferred_element_type=F32)
    squares = total * total
    lanes = squares[:, :128]
    for k in range(1, squares.shape[1] // 128):
        lanes = lanes + squares[:, 128 * k : 128 * (k + 1)]
    square_ref[...] = lanes
    hidden_ref[...] = (total * gain_ref[...]).astype(BF)


def residual_piece(scalars, attn, teacher_in, gain, blocks, step, spot, before):
    rows, depth = attn[0].shape
    tile = 256
    at = rows // tile if before else 0
    before = before or ()
    block, ins, outs = blocks
    blocks = (block, *ins, *outs)
    return pl.pallas_call(
        residual_kernel,
        grid_spec=pltpu.PrefetchScalarGridSpec(
            num_scalar_prefetch=1,
            grid=(rows // tile,),
            in_specs=[pl.BlockSpec((tile, depth), lambda i, s: (i, 0))] * 4
            + [
                pl.BlockSpec((tile, step), lambda i, s: (i, s[spot])),
                pl.BlockSpec((1, step), lambda i, s: (0, s[5])),
            ]
            + [pl.BlockSpec(memory_space=pl.ANY)] * (7 + len(before)),
            out_specs=[
                pl.BlockSpec((tile, step), lambda i, s: (i + at, 0)),
                pl.BlockSpec((tile, 128), lambda i, s: (i + at, 0)),
            ],
            scratch_shapes=[pltpu.VMEM((4, depth, step), BF), pltpu.SemaphoreType.DMA((4,))],
        ),
        out_shape=[
            jax.ShapeDtypeStruct((2 * rows, step), BF),
            jax.ShapeDtypeStruct((2 * rows, 128), F32),
        ],
        input_output_aliases={14: 0, 15: 1} if before else {},
        cost_estimate=pl.CostEstimate(
            flops=8 * rows * depth * step, bytes_accessed=8 * rows * depth + 8 * depth * step, transcendentals=0
        ),
    )(scalars, *attn, teacher_in, gain, *blocks, *before)


def target_kernel(s_ref, *refs):
    count = len(refs) - 10
    pieces = refs[:count]
    own, one, two, three, send_a, keep_a, send_b, keep_b, held, sems = refs[count:]
    i = pl.program_id(0)
    step = pieces[0].shape[1]
    width = held.shape[2]

    def copy(k, ref):
        return pltpu.make_async_copy(ref, held.at[s_ref[k]], sems.at[k])

    @pl.when(i == 0)
    def _():
        for k, ref in enumerate((own, one, two, three)):
            copy(k, ref).start()
        for k in range(4):
            copy(k, own).wait()

    sums = []
    for k in range(4):
        total = jnp.zeros((pieces[0].shape[0], width), F32)
        for p, piece in enumerate(pieces):
            total = total + jnp.dot(
                piece[...], held[k, p * step : (p + 1) * step, :], preferred_element_type=F32
            )
        sums.append(total.astype(BF))

    @pl.when(i < pl.num_programs(0) // 2)
    def _():
        send_a[:, :width] = sums[1]
        send_a[:, width:] = sums[2]
        keep_a[:, :width] = sums[0]
        keep_a[:, width:] = sums[3]

    @pl.when(i >= pl.num_programs(0) // 2)
    def _():
        send_b[:, :width] = sums[2]
        send_b[:, width:] = sums[3]
        keep_b[:, :width] = sums[0]
        keep_b[:, width:] = sums[1]


def target_parts(scalars, mine, other, blocks):
    rows, step = mine[0].shape
    depth, width = blocks[0].shape
    tile = 256
    half = rows // tile // 2
    low = pl.BlockSpec((tile, 2 * width), lambda i, s: (jnp.minimum(i, half - 1), 0))
    high = pl.BlockSpec((tile, 2 * width), lambda i, s: (jnp.maximum(i - half, 0), 0))
    return pl.pallas_call(
        target_kernel,
        grid_spec=pltpu.PrefetchScalarGridSpec(
            num_scalar_prefetch=1,
            grid=(2 * half,),
            in_specs=[pl.BlockSpec((tile, step), lambda i, s: (i, 0))] * len(mine)
            + [pl.BlockSpec((tile, step), lambda i, s: (lax.rem(i + half, 2 * half), 0))] * len(other)
            + [pl.BlockSpec(memory_space=pl.ANY)] * 4,
            out_specs=[low, low, high, high],
            scratch_shapes=[pltpu.VMEM((4, depth, width), BF), pltpu.SemaphoreType.DMA((4,))],
        ),
        out_shape=[jax.ShapeDtypeStruct((rows // 2, 2 * width), BF)] * 4,
        cost_estimate=pl.CostEstimate(
            flops=8 * rows * depth * width,
            bytes_accessed=2 * rows * depth + 8 * depth * width + 8 * rows * width,
            transcendentals=0,
        ),
    )(scalars, *mine, *other, *blocks)


def fast(
    teacher_in,
    teacher_attn,
    teacher_out_proj,
    teacher_gain,
    projection,
    student_in,
    student_attn,
    student_out_proj,
    student_gain,
    token_ids,
    row_order,
):
    students = lax.axis_size("student")
    teachers = lax.axis_size("teacher")
    rows = teacher_in.shape[0]
    piece = rows // students
    s = lax.axis_index("student")
    t = lax.axis_index("teacher")
    chip, core = s // 2, lax.rem(s, 2)
    inner = (chip == 1) | (chip == 2)
    first = core == 0
    width_t = teacher_in.shape[1] * teachers
    width_s = student_in.shape[1] * teachers

    def along(pairs):
        return [(2 * a + c, 2 * b + c) for a, b in pairs for c in range(2)]

    def line(x, *pairs):
        return lax.ppermute(x, "student", along(pairs))

    def swap(x):
        return lax.ppermute(x, "student", [(i, i ^ 1) for i in range(students)])

    def square(x, j):
        return lax.ppermute(x, "teacher", [(i, i ^ j) for i in range(teachers)])

    def halves(x, axis=-1):
        low, high = jnp.split(x, 2, axis=axis)
        return jnp.where(first, low, high), jnp.where(first, high, low)

    def ordered(mine, other, axis):
        return jnp.where(
            first, jnp.concatenate([mine, other], axis), jnp.concatenate([other, mine], axis)
        )

    def flip(x):
        half = x.shape[0] // 2
        return jnp.concatenate([x[half:], x[:half]], axis=0)

    def rows_of_both(x):
        mine, other = halves(x)
        return jnp.concatenate([mine, swap(other)], axis=0)

    def total_over(x, gate=None):
        x = x + flip(swap(x))
        others = [square(x, j) for j in range(1, teachers)]
        if gate is not None:
            *others, _ = lax.optimization_barrier((*others, gate))
        return x + others[0] + others[1] + others[2]

    def slot(q):
        j = t ^ q
        return j ^ (j >> 1)

    chips_far = (near_far(chip, 2, 1), near_far(chip, 3, 0))

    def fill(blocks, order):
        full = jnp.zeros((teachers, *blocks[0].shape), BF)
        for q, block in zip((chip, chip ^ 1, *chips_far), blocks):
            full = lax.dynamic_update_index_in_dim(full, block, order(q), 0)
        return full

    def spread(block):
        one = line(block, (0, 1), (3, 2))
        one_out = line(block, (1, 0), (2, 3))
        two = line(block, (1, 2), (2, 1))
        three = line(one, (1, 2), (2, 1))
        two_out = line(two, (1, 0), (2, 3))
        three_out = line(three, (1, 0), (2, 3))
        return block, (one, two, three), (one_out, two_out, three_out)

    def inward(block):
        one = line(block, (0, 1), (3, 2))
        two = line(block, (1, 2), (2, 1))
        three = line(one, (1, 2), (2, 1))
        return [block, one, two, three]

    attn_x, attn_y = square(teacher_attn, 1), square(teacher_attn, 2)
    out_proj_mine, out_proj_other = halves(teacher_out_proj)
    out_proj = ordered(out_proj_mine, swap(out_proj_other), 0)
    splits = NF
    step_f = out_proj.shape[1] // splits
    out_blocks = []
    for f in range(splits):
        block = out_proj[:, f * step_f : (f + 1) * step_f]
        out_blocks.append(spread(block))
    half = rows // 2
    attn_xy = jnp.concatenate([square(attn_x[:half], 2), square(attn_y[half:], 1)], axis=0)
    attn = [teacher_attn, attn_x, attn_y, attn_xy]
    attn_other = [swap(a) for a in attn]
    teacher_in_other = swap(halves(teacher_in)[1])
    live = jnp.where(token_ids != PAD_ID, 1.0, 0.0)
    live = jnp.concatenate([live, swap(live)])

    row_blocks = row_order.reshape(students, students, piece)
    neighbour = near_far(chip, 0, 3)
    sources = jnp.stack([2 * chip + core, 2 * chip + 1 - core, 2 * neighbour + core, 2 * neighbour + 1 - core])
    targets = jnp.stack([neighbour, 3 - neighbour, 3 - chip, chip])
    targets = (2 * targets[:, None] + jnp.stack([core, 1 - core])[None, :]).reshape(-1)
    chosen = row_blocks[targets[None, :], sources[:, None]] - (sources * rows)[:, None, None]
    iota = jnp.arange(rows, dtype=jnp.int32)
    select = (chosen.reshape(4, rows)[:, :, None] == iota[None, None, :]).astype(BF)

    attn_s_parts = [student_attn] + [square(student_attn, j) for j in range(1, teachers)]
    chips = jnp.stack([chip, chip ^ 1, *chips_far])
    square_lanes = jnp.zeros((2 * rows, 128), F32)
    hidden, hidden_next = [], []
    gain_row = teacher_gain.astype(F32)[None, :]
    for f in range(splits):
        scalars = jnp.concatenate(
            [t ^ chips, jnp.stack([inner.astype(jnp.int32), core * splits + f, jnp.int32(f)])]
        ).astype(jnp.int32)
        got = None
        for k, source in enumerate(((attn, teacher_in), (attn_other, teacher_in_other))):
            got = residual_piece(scalars, *source, gain_row, out_blocks[f], step_f, 5 + k, got)
        square_lanes = square_lanes + got[1]
        hidden.append(got[0])
        if f == 0:
            attn_s_parts = lax.optimization_barrier((*attn_s_parts, hidden[0]))[:-1]
            attn_s_mine = jnp.concatenate(attn_s_parts, axis=1)
            attn_s_other = swap(attn_s_mine)
        hidden_next.append(line(hidden[-1], (0, 1), (3, 2)))
    hidden_other = [swap(h) for h in hidden]
    proj = jnp.concatenate(halves(projection, 0), axis=0)
    width = proj.shape[1] // NC
    proj_blocks = []
    for j in range(NC):
        proj_blocks.append(inward(proj[:, j * width : (j + 1) * width]))

    student_out_mine, student_out_other = halves(student_out_proj)
    student_out = ordered(student_out_mine, swap(student_out_other), 0)
    student_blocks = spread(student_out)
    student_in_all = rows_of_both(student_in)

    slots = jnp.stack([slot(q) for q in (chip, chip ^ 1, 3 - chip, 3 - (chip ^ 1))]).astype(jnp.int32)

    def reduced(early, late, send_a, keep_a, send_b, keep_b):
        w = width
        got_a, got_b = square(send_a, 1), square(send_b, 2)
        got_a, got_b, _ = lax.optimization_barrier((got_a, got_b, early))
        pass_a = (keep_a[:, w:].astype(F32) + got_a[:, w:].astype(F32)).astype(BF)
        pass_b = (keep_b[:, w:].astype(F32) + got_b[:, :w].astype(F32)).astype(BF)
        last_a, last_b = square(pass_a, 2), square(pass_b, 1)
        last_a, last_b, _ = lax.optimization_barrier((last_a, last_b, late))
        return [
            keep_a[:, :w].astype(F32) + got_a[:, :w].astype(F32) + last_a.astype(F32),
            keep_b[:, :w].astype(F32) + got_b[:, w:].astype(F32) + last_b.astype(F32),
        ]

    own_parts = [target_parts(slots, hidden, hidden_other, proj_blocks[j]) for j in range(NC)]

    hidden_next_other = [swap(h) for h in hidden_next]
    next_parts = [target_parts(slots, hidden_next, hidden_next_other, proj_blocks[j]) for j in range(NC)]
    late = next_parts[-1][0]
    late_free = own_parts[-1][0]
    teacher_scale = lax.rsqrt(total_over(jnp.sum(square_lanes, axis=1), own_parts[0][0]) / width_t + epsilon)
    teacher_scale = jnp.where(live > 0, teacher_scale, -1.0)
    scale_next = line(teacher_scale, (0, 1), (3, 2))
    own_sums = [reduced(next_parts[0][0] if j else late_free, late, *p) for j, p in enumerate(own_parts)]
    scales = jnp.concatenate([teacher_scale, scale_next])[:, None]

    def scaled(x, i):
        factor = scales[i * rows : (i + 1) * rows]
        return jnp.where(factor > 0, x * factor, jnp.where(factor < 0, DEAD, 0.0)).astype(BF)

    picks, pieces = [], []
    for j in range(NC):
        sums = own_sums[j] + reduced(late, late, *next_parts[j])
        target = jnp.concatenate([scaled(x, i) for i, x in enumerate(sums)], axis=0)
        picked = lax.dot_general(
            select,
            target.reshape(4, rows, width),
            (((2,), (1,)), ((0,), (0,))),
            preferred_element_type=F32,
        ).astype(BF)
        picked = picked.reshape(4, 4, 2 * piece, width)
        far_got = line(picked[:, 1], (1, 3), (2, 0))
        mid_got = line(picked[:, 2], (1, 2), (2, 1))
        near_got = line(picked[:, 0], (1, 0), (2, 3))
        picks.append((picked, far_got, mid_got, near_got))
    last = picks[-1][0]
    attn_s = jnp.concatenate([attn_s_mine, after(attn_s_other, last)], axis=0)
    own_block, ins, outs = student_blocks
    *student_blocks, _ = lax.optimization_barrier((*ins, *outs, last))
    student_blocks = [own_block] + [
        jnp.where(inner, a, b) for a, b in zip(student_blocks[:3], student_blocks[3:])
    ]
    student_proj = fill(student_blocks, lambda q: t ^ q)
    student_res = student_in_all.astype(F32) + jnp.dot(
        attn_s, student_proj.reshape(-1, student_proj.shape[2]), preferred_element_type=F32
    )
    student_squares = jnp.sum(student_res * student_res, axis=1)
    student_scale = lax.rsqrt(total_over(student_squares) / width_s + epsilon)
    normed = student_res * student_scale[:, None]
    gain_values = halves(student_gain.astype(F32))[0][None, :]

    for picked, *got in picks:
        far_got, mid_got, near_got, _ = lax.optimization_barrier((*got, last))
        near = jnp.where(inner, picked[:, 3], near_got)
        far = jnp.where(inner, mid_got, far_got)
        low, high = near_far(chip, near, far), near_far(chip, far, near)
        both = jnp.concatenate([low[2:], low[:2], high], axis=0).reshape(4, 2, 2, piece, width)
        both = jnp.where(first, both, both[:, ::-1])
        pieces.append(both.transpose(2, 0, 1, 3, 4).reshape(2 * rows, width))

    loss_weight = 1.0 / math.sqrt(rows * students)
    inner_part = jnp.zeros((2 * rows,), F32)
    gain_part, kept = [], []
    for j, piece_j in enumerate(pieces):
        cut = slice(j * width, (j + 1) * width)
        target = piece_j.astype(F32)
        normed_j, gain_j = normed[:, cut], gain_values[:, cut]
        grad_out = jnp.where(target > 2.0**90, 0.0, (normed_j * gain_j - target) * loss_weight)
        gain_part.append(jnp.sum(grad_out * normed_j, axis=0))
        grad_norm = grad_out * gain_j
        inner_part = inner_part + jnp.sum(grad_norm * normed_j, axis=1)
        kept.append((normed_j, grad_norm))
    inner_mean = (total_over(inner_part) / width_s)[:, None]
    totals = []
    for normed_j, grad_norm in kept:
        grad_res = (student_scale[:, None] * (grad_norm - normed_j * inner_mean)).astype(BF)
        partial = lax.dot_general(
            attn_s, grad_res, (((0,), (0,)), ((), ())), preferred_element_type=F32
        ).astype(BF)
        partial = partial.reshape(teachers, -1, partial.shape[1])
        total = lax.dynamic_index_in_dim(partial, t ^ chip, 0, keepdims=False).astype(F32)
        for step in range(3, 0, -1):
            got = line(
                lax.dynamic_index_in_dim(partial, t ^ chip ^ step, 0, keepdims=False),
                *[(q, q ^ step) for q in range(4)],
            )
            total = total + got.astype(F32)
        totals.append(total)
    total = jnp.concatenate(totals, axis=1)
    gain_part = jnp.concatenate(gain_part)
    mine, other = halves(total, axis=0)
    grad_weight = ordered(mine, swap(other), 1)
    gain_part = gain_part + line(gain_part, *[(q, q ^ 1) for q in range(4)])
    gain_part = gain_part + line(gain_part, *[(q, q ^ 2) for q in range(4)])
    grad_gain = ordered(gain_part, swap(gain_part), 0)
    return (grad_weight, grad_gain)


def solution(mesh):
    placed = (
        P("student", "teacher"),
        P("student", "teacher"),
        P("student", "teacher"),
        P("teacher"),
        P("teacher", "student"),
        P("student", "teacher"),
        P("student", "teacher"),
        P("student", "teacher"),
        P("teacher"),
        P("student"),
        P(),
    )
    special = mesh.shape["student"] == 2 * mesh.shape["teacher"] == 8

    def plan(*args):
        return (fast if special else shards)(*args)

    return jax.shard_map(
        plan,
        mesh=mesh,
        in_specs=placed,
        out_specs=(P("student", "teacher"), P("teacher")),
        check_vma=False,
    )
```
